256 devices in a mesh: feat: 64 (over y, x, z_hi), mp: 4 (over z_lo, core).
Axes of the slice: x: 4, y: 4, z: 8 (z_hi: 4, z_lo: 2; z = z_hi * 2 + z_lo), core: 2. Of those that a mesh axis runs over, the one named last changes fastest.
Arguments:
- acts_in: bfloat16 [3, 512, 3584], P(None, 'feat', 'mp'), may hold values from -6 to 6
- targets: bfloat16 [3, 512, 3584], P(None, 'feat', 'mp'), may hold values from -6 to 6
- enc_weight: bfloat16 [3, 3584, 16384], P(None, 'mp', 'feat'), may hold values from -0.09375 to 0.09375
- enc_bias: float32 [3, 16384], P(None, 'feat'), may hold values from -3 to 3
- dec_weight: bfloat16 [6, 16384, 3584], P(None, 'feat', 'mp'), may hold values from -0.046875 to 0.046875
- dec_bias: float32 [3, 3584], P(None, 'mp'), may hold values from -3 to 3
Outputs:
- residual_error: bfloat16 [3, 512, 3584], P(None, 'feat', 'mp')
- grad_enc: bfloat16 [3, 3584, 16384], P(None, 'mp', 'feat')
- grad_dec: bfloat16 [6, 16384, 3584], P(None, 'feat', 'mp')
- grad_enc_bias: float32 [3, 16384], P(None, 'feat')
The draws below stay inside these ranges and needn't reach their ends.
All inputs are finite; a program needn't handle non-finite values.
Results may differ from the reference program's by a relative error of at most 0.014.
Values may be sent and summed in bfloat16 or wider, within the bound.
No kernel may reach another device: no remote copies, remote signals or barrier semaphores. Data moves between devices by JAX's collectives and lax.ppermute only.
A program may use at most 64 MiB of HBM per device.

```python
import math
import jax
import jax.numpy as jnp
from jax import lax

D = 3584
F = 16384
LAYERS = 3
PAIRS = 6
TOKENS = 512


def block_scale(rng, extent, cuts, low, largest):
    factor_of = 1.0
    for position, blocks in cuts:
        draws = jax.random.uniform(jax.random.fold_in(jax.random.fold_in(rng, 6), position), (blocks,), jnp.float32, low / len(cuts), largest / len(cuts))
        factor_of = factor_of * jnp.repeat(jnp.exp(draws), extent[position] // blocks).reshape((-1,) + (1,) * (len(extent) - 1 - position))
    return factor_of


def noise(rng, extent, spread, bound, split=(), held_as=jnp.bfloat16):
    entries = jax.random.normal(rng, extent, jnp.float32) * spread
    if len(split) > 0:
        entries = block_scale(rng, extent, split, -0.22, 0.18) * entries
    return jnp.clip(entries, min=-bound, max=bound).astype(held_as)


def setup_inputs(seed: int = 0) -> dict:
    key_of = jax.random.split(jax.random.key(seed), 7)
    return {
        "acts_in": noise(key_of[0], (LAYERS, TOKENS, D), 1.0, 6.0, ((1, 64), (2, 4))),
        "targets": noise(key_of[1], (LAYERS, TOKENS, D), 1.0, 6.0, ((1, 64), (2, 4))),
        "enc_weight": noise(key_of[2], (LAYERS, D, F), D ** -0.5, 0.09375, ((1, 4), (2, 64))),
        "enc_bias": noise(key_of[3], (LAYERS, F), 0.5, 3.0, ((1, 64),), jnp.float32),
        "dec_weight": noise(key_of[4], (PAIRS, F, D), F ** -0.5, 0.046875, ((1, 64), (2, 4))),
        "dec_bias": noise(key_of[5], (LAYERS, D), 0.5, 3.0, ((1, 4),), jnp.float32),
    }


def pair_index(source, target):
    return source * (2 * LAYERS - source + 1) // 2 + target - source

def reference(acts_in, targets, enc_weight, enc_bias, dec_weight, dec_bias):
    loss_scale = 1.0 / math.sqrt(TOKENS)
    pre_list = []
    feature_acts = []
    for layer_idx in range(LAYERS):
        pre_one = jnp.dot(acts_in[layer_idx], enc_weight[layer_idx], preferred_element_type=jnp.float32) + enc_bias[layer_idx]
        pre_list.append(pre_one)
        feature_acts.append(jnp.maximum(pre_one, 0.0).astype(jnp.bfloat16))
    errors = []
    for target in range(LAYERS):
        total = jnp.zeros((TOKENS, D), jnp.float32)
        for source in range(target + 1):
            total = total + jnp.dot(feature_acts[source], dec_weight[pair_index(source, target)], preferred_element_type=jnp.float32)
        total = total + dec_bias[target]
        errors.append((total - targets[target].astype(jnp.float32)).astype(jnp.bfloat16))
    grad_dec = []
    for source in range(LAYERS):
        for target in range(source, LAYERS):
            prod = jnp.dot(feature_acts[source].T, errors[target], preferred_element_type=jnp.float32)
            grad_dec.append((prod * loss_scale).astype(jnp.bfloat16))
    grad_enc = []
    grad_bias = []
    for source in range(LAYERS):
        grad_act = jnp.zeros((TOKENS, F), jnp.float32)
        for target in range(source, LAYERS):
            grad_act = grad_act + jnp.dot(errors[target], dec_weight[pair_index(source, target)].T, preferred_element_type=jnp.float32)
        grad_act = grad_act * loss_scale
        grad_pre = jnp.where(pre_list[source] > 0.0, grad_act, 0.0).astype(jnp.bfloat16)
        grad_enc.append(jnp.dot(acts_in[source].T, grad_pre, preferred_element_type=jnp.float32).astype(jnp.bfloat16))
        grad_bias.append(lax.optimization_barrier(jnp.sum(grad_pre.astype(jnp.float32), axis=0)))
    return (jnp.stack(errors), jnp.stack(grad_enc), jnp.stack(grad_dec), jnp.stack(grad_bias))
```

```python
import math

import jax
import jax.numpy as jnp
from jax import lax
from jax.sharding import Mesh, PartitionSpec as P

BF16 = jnp.bfloat16
F32 = jnp.float32
PLANE = ("y", "x")
FEAT = ("y", "x", "zh")
MP = ("zl", "core")


def pair_index(source, target, layers):
    return source * (2 * layers - source + 1) // 2 + target - source


def swap(value, axis):
    return lax.ppermute(value, axis, [(0, 1), (1, 0)])


def halves_add(value, axis):
    rows = value.shape[0] // 2
    me = lax.axis_index(axis)
    mine = lax.dynamic_slice_in_dim(value, me * rows, rows, 0)
    theirs = lax.dynamic_slice_in_dim(value, (1 - me) * rows, rows, 0)
    return mine.astype(F32) + swap(theirs, axis).astype(F32)


def halves_join(value, axis):
    got = swap(value, axis)
    first = lax.axis_index(axis) == 0
    return jnp.concatenate([jnp.where(first, value, got), jnp.where(first, got, value)], axis=0)


def gather_plane(value):
    members = lax.axis_size("y") * lax.axis_size("x")
    copies = jnp.broadcast_to(value[None], (members,) + value.shape)
    got = lax.all_to_all(copies, PLANE, split_axis=0, concat_axis=0, tiled=True)
    return got.reshape(-1, value.shape[-1])


def gather_feat(value):
    return gather_plane(lax.all_gather(value, "zh", axis=0, tiled=True))


def scatter_sum(partial, axes, members):
    blocks = partial.reshape(members, -1, partial.shape[-1])
    got = lax.all_to_all(blocks, axes, split_axis=0, concat_axis=0, tiled=True)
    return jnp.sum(got.astype(F32), axis=0)


def on_device(acts_in, targets, enc_weight, enc_bias, dec_weight, dec_bias):
    layers = enc_weight.shape[0]
    plane = lax.axis_size("y") * lax.axis_size("x")
    zhs = lax.axis_size("zh")
    tokens_all = acts_in.shape[1] * plane * zhs
    loss_scale = 1.0 / math.sqrt(tokens_all)

    acts = [gather_feat(acts_in[l]) for l in range(layers)]
    pre_own, feature = [], []
    for l in range(layers):
        partial = jnp.dot(acts[l], enc_weight[l], preferred_element_type=F32)
        pre = halves_add(halves_add(partial, "core"), "zl") + enc_bias[l][None, :]
        pre_own.append(pre)
        own = jnp.maximum(pre, 0.0).astype(BF16)
        feature.append(halves_join(halves_join(own, "zl"), "core"))

    errors, err_all = [], []
    for target in range(layers):
        total = jnp.zeros((tokens_all, acts_in.shape[2]), F32)
        for source in range(target + 1):
            total = total + jnp.dot(
                feature[source], dec_weight[pair_index(source, target, layers)], preferred_element_type=F32
            )
        part = scatter_sum(total.astype(BF16), PLANE, plane)
        recon = scatter_sum(part.astype(BF16), "zh", zhs)
        error = (recon + dec_bias[target][None, :] - targets[target].astype(F32)).astype(BF16)
        errors.append(error)
        err_all.append(gather_feat(error))

    grad_dec = {}
    grad_enc = [None] * layers
    grad_bias = [None] * layers
    for source in reversed(range(layers)):
        grad_act = jnp.zeros((tokens_all, enc_weight.shape[2]), F32)
        for target in range(source, layers):
            pair = pair_index(source, target, layers)
            prod = jnp.einsum("tf,td->fd", feature[source], err_all[target], preferred_element_type=F32)
            grad_dec[pair] = (prod * loss_scale).astype(BF16)
            grad_act = grad_act + jnp.einsum(
                "td,fd->tf", err_all[target], dec_weight[pair], preferred_element_type=F32
            )
        half = halves_add((grad_act * loss_scale).astype(BF16), "core")
        summed = halves_add(half.astype(BF16), "zl")
        own = jnp.where(pre_own[source] > 0.0, summed, 0.0).astype(BF16)
        grad_pre = halves_join(halves_join(own, "zl"), "core")
        grad_enc[source] = jnp.einsum("td,tf->df", acts[source], grad_pre, preferred_element_type=F32).astype(BF16)
        grad_bias[source] = jnp.sum(grad_pre.astype(F32), axis=0)
    return (
        jnp.stack(errors),
        jnp.stack(grad_enc),
        jnp.stack([grad_dec[pair] for pair in range(len(grad_dec))]),
        jnp.stack(grad_bias),
    )


def solution(mesh):
    fine = Mesh(mesh.devices.reshape(4, 4, 4, 2, 2), FEAT + MP)
    return jax.shard_map(
        on_device,
        mesh=fine,
        in_specs=(
            P(None, FEAT, MP),
            P(None, FEAT, MP),
            P(None, MP, FEAT),
            P(None, FEAT),
            P(None, FEAT, MP),
            P(None, MP),
        ),
        out_specs=(
            P(None, FEAT, MP),
            P(None, MP, FEAT),
            P(None, FEAT, MP),
            P(None, FEAT),
        ),
        check_vma=False,
    )
```

```python
import math

import jax
import jax.numpy as jnp
from jax import lax
from jax.sharding import Mesh, PartitionSpec as P

BF16 = jnp.bfloat16
F32 = jnp.float32
FEAT = ("y", "x", "zh")
MP = ("zl", "core")
RING = 4


def pair_index(source, target, layers):
    return source * (2 * layers - source + 1) // 2 + target - source


def shift(value, axis, by):
    return lax.ppermute(value, axis, [(i, (i + by) % RING) for i in range(RING)])


def swap(value, axis):
    return lax.ppermute(value, axis, [(0, 1), (1, 0)])


def halves_add(value, axis):
    rows = value.shape[1] // 2
    me = lax.axis_index(axis)
    mine = lax.dynamic_slice_in_dim(value, me * rows, rows, 1)
    theirs = lax.dynamic_slice_in_dim(value, (1 - me) * rows, rows, 1)
    return mine.astype(F32) + swap(theirs, axis).astype(F32)


def halves_join(value, axis):
    got = swap(value, axis)
    first = lax.axis_index(axis) == 0
    return jnp.concatenate([jnp.where(first, value, got), jnp.where(first, got, value)], axis=1)


def spread(value, axis):
    return [value] + [shift(value, axis, s) for s in range(1, RING)]


def fold(pieces, axis):
    total = pieces[0].astype(F32)
    for s in range(1, RING):
        total = total + shift(pieces[s].astype(BF16), axis, -s).astype(F32)
    return total


def rows_of(value, count):
    n = value.shape[1] // count
    return [value[:, i * n : (i + 1) * n] for i in range(count)]


def gather_feat(value):
    zs = spread(value, "zh")
    a = jnp.concatenate(zs[:2], axis=1)
    b = jnp.concatenate(zs[2:], axis=1)
    a, b = lax.optimization_barrier((a, b))
    a, b = spread(a, "x"), spread(b, "y")
    a, b = jnp.concatenate(a, axis=1), jnp.concatenate(b, axis=1)
    a, b = lax.optimization_barrier((a, b))
    return jnp.concatenate(spread(a, "y") + spread(b, "x"), axis=1)


def scatter_feat(value):
    pieces = rows_of(value, 2 * RING)
    a, b = lax.optimization_barrier((fold(pieces[:RING], "y"), fold(pieces[RING:], "x")))
    a, b = lax.optimization_barrier((fold(rows_of(a, RING), "x"), fold(rows_of(b, RING), "y")))
    return fold(rows_of(a, 2) + rows_of(b, 2), "zh")


def on_device(acts_in, targets, enc_weight, enc_bias, dec_weight, dec_bias):
    layers = enc_weight.shape[0]
    acts = gather_feat(acts_in)
    loss_scale = 1.0 / math.sqrt(acts.shape[1])

    partial = jnp.einsum("ltd,ldf->ltf", acts, enc_weight, preferred_element_type=F32)
    pre_own = halves_add(halves_add(partial, "core"), "zl") + enc_bias[:, None, :]
    own = jnp.maximum(pre_own, 0.0).astype(BF16)
    feature = halves_join(halves_join(own, "zl"), "core")

    totals = []
    for target in range(layers):
        total = 0.0
        for source in range(target + 1):
            total = total + jnp.dot(
                feature[source], dec_weight[pair_index(source, target, layers)], preferred_element_type=F32
            )
        totals.append(total.astype(BF16))
    recon = scatter_feat(jnp.stack(totals))
    errors = (recon + dec_bias[:, None, :] - targets.astype(F32)).astype(BF16)
    err_all = gather_feat(errors)

    grad_dec = {}
    grad_act = []
    for source in range(layers):
        total = 0.0
        for target in range(source, layers):
            pair = pair_index(source, target, layers)
            total = total + jnp.einsum("td,fd->tf", err_all[target], dec_weight[pair], preferred_element_type=F32)
            prod = jnp.einsum("tf,td->fd", feature[source], err_all[target], preferred_element_type=F32)
            grad_dec[pair] = (prod * loss_scale).astype(BF16)
        grad_act.append((total * loss_scale).astype(BF16))
    half = halves_add(jnp.stack(grad_act), "core")
    summed = halves_add(half.astype(BF16), "zl")
    own = jnp.where(pre_own > 0.0, summed, 0.0).astype(BF16)
    grad_pre = halves_join(halves_join(own, "zl"), "core")
    grad_enc = jnp.einsum("ltd,ltf->ldf", acts, grad_pre, preferred_element_type=F32).astype(BF16)
    grad_bias = jnp.sum(grad_pre.astype(F32), axis=1)
    return (errors, grad_enc, jnp.stack([grad_dec[pair] for pair in range(len(grad_dec))]), grad_bias)


def solution(mesh):
    fine = Mesh(mesh.devices.reshape(RING, RING, RING, 2, 2), FEAT + MP)
    return jax.shard_map(
        on_device,
        mesh=fine,
        in_specs=(
            P(None, FEAT, MP),
            P(None, FEAT, MP),
            P(None, MP, FEAT),
            P(None, FEAT),
            P(None, FEAT, MP),
            P(None, MP),
        ),
        out_specs=(
            P(None, FEAT, MP),
            P(None, MP, FEAT),
            P(None, FEAT, MP),
            P(None, FEAT),
        ),
        check_vma=False,
    )
```

```python
import math

import jax
import jax.numpy as jnp
from jax import lax
from jax.sharding import Mesh, PartitionSpec as P

BF16 = jnp.bfloat16
F32 = jnp.float32
FEAT = ("y", "x", "zh")
MP = ("zl", "core")
RING = 4


def pair_index(source, target, layers):
    return source * (2 * layers - source + 1) // 2 + target - source


def shift(value, stage, by):
    if stage == "zh":
        return lax.ppermute(value, "zh", [(i, (i + by) % RING) for i in range(RING)])
    pairs = []
    for y in range(RING):
        for x in range(RING):
            for core in range(2):
                if (stage == "first") == (core == 0):
                    to = (y, (x + by) % RING)
                else:
                    to = ((y + by) % RING, x)
                pairs.append(((y * RING + x) * 2 + core, (to[0] * RING + to[1]) * 2 + core))
    return lax.ppermute(value, ("y", "x", "core"), pairs)


def swap(value, axis):
    return lax.ppermute(value, axis, [(0, 1), (1, 0)])


def flip(value):
    lead, rows, width = value.shape
    return value.reshape(lead, RING, RING, rows // RING**2, width).swapaxes(1, 2).reshape(value.shape)


def core_add(value):
    lead, rows, width = value.shape
    blocks = value.reshape(lead, RING**2, 2, rows // (2 * RING**2), width)
    me = lax.axis_index("core")
    mine = lax.dynamic_index_in_dim(blocks, me, 2, keepdims=False).reshape(lead, rows // 2, width)
    theirs = lax.dynamic_index_in_dim(blocks, 1 - me, 2, keepdims=False).reshape(lead, rows // 2, width)
    return mine.astype(F32) + flip(swap(theirs, "core")).astype(F32)


def core_join(value):
    lead, rows, width = value.shape
    got = flip(swap(value, "core"))
    first = lax.axis_index("core") == 0
    split = (lead, RING**2, 1, rows // RING**2, width)
    halves = [jnp.where(first, value, got).reshape(split), jnp.where(first, got, value).reshape(split)]
    return jnp.concatenate(halves, axis=2).reshape(lead, 2 * rows, width)


def chip_add(value):
    rows = value.shape[1] // 2
    me = lax.axis_index("zl")
    mine = lax.dynamic_slice_in_dim(value, me * rows, rows, 1)
    theirs = lax.dynamic_slice_in_dim(value, (1 - me) * rows, rows, 1)
    return mine.astype(F32) + swap(theirs, "zl").astype(F32)


def chip_join(value):
    got = swap(value, "zl")
    first = lax.axis_index("zl") == 0
    return jnp.concatenate([jnp.where(first, value, got), jnp.where(first, got, value)], axis=1)


def spread(value, stage):
    slots = {s: shift(value, stage, s) for s in (2, 1, 3)}
    return jnp.concatenate([value] + [slots[s] for s in range(1, RING)], axis=1)


def fold(value, stage):
    n = value.shape[1] // RING
    pieces = [value[:, s * n : (s + 1) * n] for s in range(RING)]
    total = pieces[0].astype(F32)
    for s in range(1, RING):
        total = total + shift(pieces[s].astype(BF16), stage, -s).astype(F32)
    return total


def gather_feat(value):
    return spread(spread(spread(value, "zh"), "first"), "second")


def scatter_feat(value):
    return fold(fold(fold(value, "second"), "first"), "zh")


def on_device(acts_in, targets, enc_weight, enc_bias, dec_weight, dec_bias):
    layers = enc_weight.shape[0]
    acts = gather_feat(acts_in)
    loss_scale = 1.0 / math.sqrt(acts.shape[1])

    partial = jnp.einsum("ltd,ldf->ltf", acts, enc_weight, preferred_element_type=F32)
    pre_own = chip_add(core_add(partial)) + enc_bias[:, None, :]
    own = jnp.maximum(pre_own, 0.0).astype(BF16)
    feature = core_join(chip_join(own))

    totals = []
    for target in range(layers):
        total = 0.0
        for source in range(target + 1):
            total = total + jnp.dot(
                feature[source], dec_weight[pair_index(source, target, layers)], preferred_element_type=F32
            )
        totals.append(total.astype(BF16))
    recon = scatter_feat(jnp.stack(totals))
    errors = (recon + dec_bias[:, None, :] - targets.astype(F32)).astype(BF16)
    err_all = gather_feat(errors)

    grad_dec = {}
    grad_act = []
    for source in range(layers):
        total = 0.0
        for target in range(source, layers):
            pair = pair_index(source, target, layers)
            total = total + jnp.einsum("td,fd->tf", err_all[target], dec_weight[pair], preferred_element_type=F32)
            prod = jnp.einsum("tf,td->fd", feature[source], err_all[target], preferred_element_type=F32)
            grad_dec[pair] = (prod * loss_scale).astype(BF16)
        grad_act.append((total * loss_scale).astype(BF16))
    half = core_add(jnp.stack(grad_act))
    summed = chip_add(half.astype(BF16))
    own = jnp.where(pre_own > 0.0, summed, 0.0).astype(BF16)
    grad_pre = core_join(chip_join(own))
    grad_enc = jnp.einsum("ltd,ltf->ldf", acts, grad_pre, preferred_element_type=F32).astype(BF16)
    grad_bias = jnp.sum(grad_pre.astype(F32), axis=1)
    return (errors, grad_enc, jnp.stack([grad_dec[pair] for pair in range(len(grad_dec))]), grad_bias)


def solution(mesh):
    fine = Mesh(mesh.devices.reshape(RING, RING, RING, 2, 2), FEAT + MP)
    return jax.shard_map(
        on_device,
        mesh=fine,
        in_specs=(
            P(None, FEAT, MP),
            P(None, FEAT, MP),
            P(None, MP, FEAT),
            P(None, FEAT),
            P(None, FEAT, MP),
            P(None, MP),
        ),
        out_specs=(
            P(None, FEAT, MP),
            P(None, MP, FEAT),
            P(None, FEAT, MP),
            P(None, FEAT),
        ),
        check_vma=False,
    )
```

```python
import math

import jax
import jax.numpy as jnp
from jax import lax
from jax.sharding import Mesh, PartitionSpec as P

BF16 = jnp.bfloat16
F32 = jnp.float32
FEAT = ("y", "x", "zh")
MP = ("zl", "core")
RING = 4


def pair_index(source, target, layers):
    return source * (2 * layers - source + 1) // 2 + target - source


def exchange(value, stage, pattern):
    to = [i ^ 1 if pattern == 1 else 3 - i for i in range(RING)]
    if stage == "zh":
        return lax.ppermute(value, "zh", list(enumerate(to)))
    pairs = []
    for y in range(RING):
        for x in range(RING):
            for core in range(2):
                ty, tx = (y, to[x]) if (stage == "first") == (core == 0) else (to[y], x)
                pairs.append(((y * RING + x) * 2 + core, (ty * RING + tx) * 2 + core))
    return lax.ppermute(value, ("y", "x", "core"), pairs)


def swap(value, axis):
    return lax.ppermute(value, axis, [(0, 1), (1, 0)])


def flip(value):
    lead, rows, width = value.shape
    return value.reshape(lead, RING, RING, rows // RING**2, width).swapaxes(1, 2).reshape(value.shape)


def core_add(value):
    lead, rows, width = value.shape
    blocks = value.reshape(lead, RING**2, 2, rows // (2 * RING**2), width)
    me = lax.axis_index("core")
    mine = lax.dynamic_index_in_dim(blocks, me, 2, keepdims=False).reshape(lead, rows // 2, width)
    theirs = lax.dynamic_index_in_dim(blocks, 1 - me, 2, keepdims=False).reshape(lead, rows // 2, width)
    return mine.astype(F32) + flip(swap(theirs, "core")).astype(F32)


def core_join(value):
    lead, rows, width = value.shape
    got = flip(swap(value, "core"))
    first = lax.axis_index("core") == 0
    split = (lead, RING**2, 1, rows // RING**2, width)
    halves = [jnp.where(first, value, got).reshape(split), jnp.where(first, got, value).reshape(split)]
    return jnp.concatenate(halves, axis=2).reshape(lead, 2 * rows, width)


def chip_add(value):
    rows = value.shape[1] // 2
    me = lax.axis_index("zl")
    mine = lax.dynamic_slice_in_dim(value, me * rows, rows, 1)
    theirs = lax.dynamic_slice_in_dim(value, (1 - me) * rows, rows, 1)
    return mine.astype(F32) + swap(theirs, "zl").astype(F32)


def chip_join(value):
    got = swap(value, "zl")
    first = lax.axis_index("zl") == 0
    return jnp.concatenate([jnp.where(first, value, got), jnp.where(first, got, value)], axis=1)


def double(value, stage):
    pair = jnp.concatenate([value, exchange(value, stage, 1)], axis=1)
    return lax.optimization_barrier(jnp.concatenate([pair, exchange(pair, stage, 2)], axis=1))


def halve(value, stage):
    for pattern in (2, 1):
        n = value.shape[1] // 2
        got = exchange(value[:, n:].astype(BF16), stage, pattern)
        value = value[:, :n].astype(F32) + got.astype(F32)
    return value


def double_wide(value):
    stage, n = "second", value.shape[1] // 2
    one, two = exchange(value, stage, 1), exchange(value, stage, 2)
    relay = [exchange(two[:, :n], stage, 1), exchange(one[:, n:], stage, 2)]
    return jnp.concatenate([value, one, two] + relay, axis=1)


def halve_wide(value):
    stage, n = "second", value.shape[1] // 8
    own, one, two, across = (value[:, i * 2 * n : (i + 1) * 2 * n] for i in range(4))
    for_two = exchange(across[:, :n], stage, 1)
    for_one = exchange(across[:, n:], stage, 2)
    two = jnp.concatenate([(two[:, :n].astype(F32) + for_two.astype(F32)).astype(BF16), two[:, n:]], axis=1)
    one = jnp.concatenate([one[:, :n], (one[:, n:].astype(F32) + for_one.astype(F32)).astype(BF16)], axis=1)
    one, two = lax.optimization_barrier((one, two))
    return own.astype(F32) + exchange(two, stage, 2).astype(F32) + exchange(one, stage, 1).astype(F32)


def gather_feat(value):
    return double_wide(double(double(value, "zh"), "first"))


def scatter_feat(value):
    return halve(halve(halve_wide(value), "first"), "zh")


def on_device(acts_in, targets, enc_weight, enc_bias, dec_weight, dec_bias):
    layers = enc_weight.shape[0]
    acts = gather_feat(acts_in)
    loss_scale = 1.0 / math.sqrt(acts.shape[1])

    partial = jnp.einsum("ltd,ldf->ltf", acts, enc_weight, preferred_element_type=F32)
    pre_own = chip_add(core_add(partial)) + enc_bias[:, None, :]
    own = jnp.maximum(pre_own, 0.0).astype(BF16)
    feature = core_join(chip_join(own))

    totals = []
    for target in range(layers):
        total = 0.0
        for source in range(target + 1):
            total = total + jnp.dot(
                feature[source], dec_weight[pair_index(source, target, layers)], preferred_element_type=F32
            )
        totals.append(total.astype(BF16))
    recon = scatter_feat(jnp.stack(totals))
    errors = (recon + dec_bias[:, None, :] - targets.astype(F32)).astype(BF16)
    err_all = gather_feat(errors)

    grad_dec = {}
    grad_act = []
    for source in range(layers):
        total = 0.0
        for target in range(source, layers):
            pair = pair_index(source, target, layers)
            total = total + jnp.einsum("td,fd->tf", err_all[target], dec_weight[pair], preferred_element_type=F32)
            prod = jnp.einsum("tf,td->fd", feature[source], err_all[target], preferred_element_type=F32)
            grad_dec[pair] = (prod * loss_scale).astype(BF16)
        grad_act.append((total * loss_scale).astype(BF16))
    half = core_add(jnp.stack(grad_act))
    summed = chip_add(half.astype(BF16))
    own = jnp.where(pre_own > 0.0, summed, 0.0).astype(BF16)
    grad_pre = core_join(chip_join(own))
    grad_enc = jnp.einsum("ltd,ltf->ldf", acts, grad_pre, preferred_element_type=F32).astype(BF16)
    grad_bias = jnp.sum(grad_pre.astype(F32), axis=1)
    return (errors, grad_enc, jnp.stack([grad_dec[pair] for pair in range(len(grad_dec))]), grad_bias)


def solution(mesh):
    fine = Mesh(mesh.devices.reshape(RING, RING, RING, 2, 2), FEAT + MP)
    return jax.shard_map(
        on_device,
        mesh=fine,
        in_specs=(
            P(None, FEAT, MP),
            P(None, FEAT, MP),
            P(None, MP, FEAT),
            P(None, FEAT),
            P(None, FEAT, MP),
            P(None, MP),
        ),
        out_specs=(
            P(None, FEAT, MP),
            P(None, MP, FEAT),
            P(None, FEAT, MP),
            P(None, FEAT),
        ),
        check_vma=False,
    )
```

```python
import math

import jax
import jax.numpy as jnp
from jax import lax
from jax.sharding import Mesh, PartitionSpec as P

BF16 = jnp.bfloat16
F32 = jnp.float32
FEAT = ("y", "x", "zh")
MP = ("zl", "core")
PLANE = ("y", "x", "core")
RING = 4


def pair_index(source, target, layers):
    return source * (2 * layers - source + 1) // 2 + target - source


def ring_of(y, x, core, stage):
    return (x, lambda to: (y, to)) if (stage == "first") == (core == 0) else (y, lambda to: (to, x))


def plane_index(y, x, core):
    return (y * RING + x) * 2 + core


def shift_wide(value, by):
    pairs = []
    for y in range(RING):
        for x in range(RING):
            for core in range(2):
                at, move = ring_of(y, x, core, "second")
                pairs.append((plane_index(y, x, core), plane_index(*move((at + by) % RING), core)))
    return lax.ppermute(value, PLANE, pairs)


def trade(value, stage):
    if stage == "zh":
        return lax.all_to_all(value, "zh", split_axis=0, concat_axis=0, tiled=True)
    groups = [[plane_index(y, x, 0) for x in range(RING)] for y in range(RING)]
    groups += [[plane_index(y, x, 1) for y in range(RING)] for x in range(RING)]
    return lax.all_to_all(value, PLANE, split_axis=0, concat_axis=0, axis_index_groups=groups, tiled=True)


def wide_position():
    return jnp.where(lax.axis_index("core") == 0, lax.axis_index("y"), lax.axis_index("x"))


def swap(value, axis):
    return lax.ppermute(value, axis, [(0, 1), (1, 0)])


def flip(value):
    lead, rows, width = value.shape
    return value.reshape(lead, RING, RING, rows // RING**2, width).swapaxes(1, 2).reshape(value.shape)


def core_add(value):
    lead, rows, width = value.shape
    blocks = value.reshape(lead, RING**2, 2, rows // (2 * RING**2), width)
    me = lax.axis_index("core")
    mine = lax.dynamic_index_in_dim(blocks, me, 2, keepdims=False).reshape(lead, rows // 2, width)
    theirs = lax.dynamic_index_in_dim(blocks, 1 - me, 2, keepdims=False).reshape(lead, rows // 2, width)
    return mine.astype(F32) + flip(swap(theirs, "core")).astype(F32)


def core_join(value):
    lead, rows, width = value.shape
    got = flip(swap(value, "core"))
    first = lax.axis_index("core") == 0
    split = (lead, RING**2, 1, rows // RING**2, width)
    halves = [jnp.where(first, value, got).reshape(split), jnp.where(first, got, value).reshape(split)]
    return jnp.concatenate(halves, axis=2).reshape(lead, 2 * rows, width)


def spread(value, stage):
    return lax.optimization_barrier(trade(jnp.broadcast_to(value[None], (RING,) + value.shape), stage))


def fold(value, stage):
    return jnp.sum(trade(value.astype(BF16), stage).astype(F32), axis=0)


def by_layer(blocks):
    return jnp.moveaxis(blocks, 2, 0).reshape(blocks.shape[2], -1, blocks.shape[-1])


def spread_wide(value, later=None):
    lead, n, width = value.shape
    me = wide_position()
    full = jnp.zeros((lead, RING * n, width), value.dtype)
    full = lax.dynamic_update_slice_in_dim(full, value, me * n, 1)
    got = {s: shift_wide(value, s) for s in (2, 1, 3)}
    if later is not None:
        got[2], later = lax.optimization_barrier((got[2], later))
    for s in (1, 3, 2):
        full = lax.dynamic_update_slice_in_dim(full, got[s], (me - s) % RING * n, 1)
    return full, later


def fold_wide(value):
    n = value.shape[1] // RING
    me = wide_position()
    piece = lambda s: lax.dynamic_slice_in_dim(value, (me + s) % RING * n, n, 1)
    got = {s: shift_wide(piece(s), s) for s in (2, 1, 3)}
    return piece(0).astype(F32) + got[1].astype(F32) + got[3].astype(F32) + got[2].astype(F32)


def on_device(acts_in, targets, enc_weight, enc_bias, dec_weight, dec_bias):
    layers = enc_weight.shape[0]
    early, late = range(0, 1), range(1, layers)
    acts_part = spread(spread(acts_in, "zh"), "first")
    loss_scale = 1.0 / math.sqrt(acts_in.shape[1] * RING**3)

    acts, half, feature = {}, {}, {}
    for batch in (early, late):
        span = slice(batch.start, batch.stop)
        acts[batch], _ = spread_wide(by_layer(acts_part[:, :, span]))
        partial = jnp.einsum("ltd,ldf->ltf", acts[batch], enc_weight[span], preferred_element_type=F32)
        mine = core_add(partial)
        pre = mine + swap(mine, "zl") + enc_bias[span][:, None, :]
        half[batch] = jnp.maximum(pre, 0.0).astype(BF16)
        joined = core_join(half[batch])
        for i, layer in enumerate(batch):
            feature[layer] = joined[i]

    folded = []
    for batch in (early, late):
        totals = []
        for target in batch:
            total = 0.0
            for source in range(target + 1):
                total = total + jnp.dot(
                    feature[source], dec_weight[pair_index(source, target, layers)], preferred_element_type=F32
                )
            totals.append(total.astype(BF16))
        folded.append(fold_wide(jnp.stack(totals)).astype(BF16))
    blocks = jnp.concatenate(folded, axis=0).reshape(layers, RING, RING, -1, acts_in.shape[2])
    recon = fold(fold(jnp.moveaxis(blocks, 0, 2), "first"), "zh")
    errors = (recon + dec_bias[:, None, :] - targets.astype(F32)).astype(BF16)

    err_part = spread(spread(errors, "zh"), "first")
    err_all, grad_dec, grad_enc, grad_bias = {}, {}, {}, {}
    waiting = by_layer(err_part[:, :, : late.start])
    for batch in (late, early):
        if batch == late:
            err, waiting = spread_wide(by_layer(err_part[:, :, late.start :]), waiting)
        else:
            err, _ = spread_wide(waiting)
        err_all[batch] = err
        sums = []
        for source in batch:
            total = 0.0
            for part in (early, late):
                first = max(source, part.start)
                if first >= part.stop:
                    continue
                pairs = slice(pair_index(source, first, layers), pair_index(source, part.stop - 1, layers) + 1)
                got = err_all[part][first - part.start :]
                total = total + jnp.einsum("ltd,lfd->tf", got, dec_weight[pairs], preferred_element_type=F32)
                prod = jnp.einsum("tf,ltd->lfd", feature[source], got, preferred_element_type=F32)
                grad_dec[pairs.start] = (prod * loss_scale).astype(BF16)
            sums.append((total * loss_scale).astype(BF16))
        mine = core_add(jnp.stack(sums)).astype(BF16)
        summed = mine.astype(F32) + swap(mine, "zl").astype(F32)
        grad_pre = core_join(jnp.where(half[batch] > 0.0, summed, 0.0).astype(BF16))
        grad_enc[batch] = jnp.einsum("ltd,ltf->ldf", acts[batch], grad_pre, preferred_element_type=F32).astype(BF16)
        grad_bias[batch] = jnp.sum(grad_pre.astype(F32), axis=1)
    return (
        errors,
        jnp.concatenate([grad_enc[early], grad_enc[late]], axis=0),
        jnp.concatenate([grad_dec[pair] for pair in sorted(grad_dec)], axis=0),
        jnp.concatenate([grad_bias[early], grad_bias[late]], axis=0),
    )


def solution(mesh):
    fine = Mesh(mesh.devices.reshape(RING, RING, RING, 2, 2), FEAT + MP)
    return jax.shard_map(
        on_device,
        mesh=fine,
        in_specs=(
            P(None, FEAT, MP),
            P(None, FEAT, MP),
            P(None, MP, FEAT),
            P(None, FEAT),
            P(None, FEAT, MP),
            P(None, MP),
        ),
        out_specs=(
            P(None, FEAT, MP),
            P(None, MP, FEAT),
            P(None, FEAT, MP),
            P(None, FEAT),
        ),
        check_vma=False,
    )
```

```python
import math

import jax
import jax.numpy as jnp
from jax import lax
from jax.sharding import Mesh, PartitionSpec as P

BF16 = jnp.bfloat16
F32 = jnp.float32
FEAT = ("y", "x", "zh")
MP = ("zl", "core")
RING = 4


def pair_index(source, target, layers):
    return source * (2 * layers - source + 1) // 2 + target - source


def shift(value, stage, by):
    if stage == "zh":
        return lax.ppermute(value, "zh", [(i, (i + by) % RING) for i in range(RING)])
    pairs = []
    for y in range(RING):
        for x in range(RING):
            for core in range(2):
                if (stage == "first") == (core == 0):
                    to = (y, (x + by) % RING)
                else:
                    to = ((y + by) % RING, x)
                pairs.append(((y * RING + x) * 2 + core, (to[0] * RING + to[1]) * 2 + core))
    return lax.ppermute(value, ("y", "x", "core"), pairs)


def swap(value, axis):
    return lax.ppermute(value, axis, [(0, 1), (1, 0)])


def flip(value):
    lead, rows, width = value.shape
    return value.reshape(lead, RING, RING, rows // RING**2, width).swapaxes(1, 2).reshape(value.shape)


def core_add(value):
    lead, rows, width = value.shape
    blocks = value.reshape(lead, RING**2, 2, rows // (2 * RING**2), width)
    me = lax.axis_index("core")
    mine = lax.dynamic_index_in_dim(blocks, me, 2, keepdims=False).reshape(lead, rows // 2, width)
    theirs = lax.dynamic_index_in_dim(blocks, 1 - me, 2, keepdims=False).reshape(lead, rows // 2, width)
    return mine.astype(F32) + flip(swap(theirs, "core")).astype(F32)


def core_join(value):
    lead, rows, width = value.shape
    got = flip(swap(value, "core"))
    first = lax.axis_index("core") == 0
    split = (lead, RING**2, 1, rows // RING**2, width)
    halves = [jnp.where(first, value, got).reshape(split), jnp.where(first, got, value).reshape(split)]
    return jnp.concatenate(halves, axis=2).reshape(lead, 2 * rows, width)


def chip_add(value):
    rows = value.shape[1] // 2
    me = lax.axis_index("zl")
    mine = lax.dynamic_slice_in_dim(value, me * rows, rows, 1)
    theirs = lax.dynamic_slice_in_dim(value, (1 - me) * rows, rows, 1)
    return mine.astype(F32) + swap(theirs, "zl").astype(F32)


def chip_join(value):
    got = swap(value, "zl")
    first = lax.axis_index("zl") == 0
    return jnp.concatenate([jnp.where(first, value, got), jnp.where(first, got, value)], axis=1)


def spread(value, stage):
    slots = {s: shift(value, stage, s) for s in (2, 1, 3)}
    return lax.optimization_barrier(jnp.concatenate([value] + [slots[s] for s in range(1, RING)], axis=1))


def fold(value, stage):
    n = value.shape[1] // RING
    pieces = [value[:, s * n : (s + 1) * n] for s in range(RING)]
    total = pieces[0].astype(F32)
    for s in range(1, RING):
        total = total + shift(pieces[s].astype(BF16), stage, -s).astype(F32)
    return total


def gather_feat(value):
    return spread(spread(spread(value, "zh"), "first"), "second")


def scatter_feat(value):
    return fold(fold(fold(value, "second"), "first"), "zh")


def on_device(acts_in, targets, enc_weight, enc_bias, dec_weight, dec_bias):
    layers = enc_weight.shape[0]
    acts = gather_feat(acts_in)
    loss_scale = 1.0 / math.sqrt(acts.shape[1])

    partial = jnp.einsum("ltd,ldf->ltf", acts, enc_weight, preferred_element_type=F32)
    pre_own = chip_add(core_add(partial)) + enc_bias[:, None, :]
    half_feature = chip_join(jnp.maximum(pre_own, 0.0).astype(BF16))
    feature = core_join(half_feature)

    totals = []
    for target in range(layers):
        total = 0.0
        for source in range(target + 1):
            total = total + jnp.dot(
                feature[source], dec_weight[pair_index(source, target, layers)], preferred_element_type=F32
            )
        totals.append(total.astype(BF16))
    recon = scatter_feat(jnp.stack(totals))
    errors = (recon + dec_bias[:, None, :] - targets.astype(F32)).astype(BF16)
    err_all = gather_feat(errors)

    grad_dec = {}
    grad_act = []
    for source in range(layers):
        total = 0.0
        for target in range(source, layers):
            pair = pair_index(source, target, layers)
            total = total + jnp.einsum("td,fd->tf", err_all[target], dec_weight[pair], preferred_element_type=F32)
            prod = jnp.einsum("tf,td->fd", feature[source], err_all[target], preferred_element_type=F32)
            grad_dec[pair] = (prod * loss_scale).astype(BF16)
        grad_act.append((total * loss_scale).astype(BF16))
    half = core_add(jnp.stack(grad_act)).astype(BF16)
    summed = half.astype(F32) + swap(half, "zl").astype(F32)
    grad_pre = core_join(jnp.where(half_feature > 0.0, summed, 0.0).astype(BF16))
    grad_enc = jnp.einsum("ltd,ltf->ldf", acts, grad_pre, preferred_element_type=F32).astype(BF16)
    grad_bias = jnp.sum(grad_pre.astype(F32), axis=1)
    return (errors, grad_enc, jnp.stack([grad_dec[pair] for pair in range(len(grad_dec))]), grad_bias)


def solution(mesh):
    fine = Mesh(mesh.devices.reshape(RING, RING, RING, 2, 2), FEAT + MP)
    return jax.shard_map(
        on_device,
        mesh=fine,
        in_specs=(
            P(None, FEAT, MP),
            P(None, FEAT, MP),
            P(None, MP, FEAT),
            P(None, FEAT),
            P(None, FEAT, MP),
            P(None, MP),
        ),
        out_specs=(
            P(None, FEAT, MP),
            P(None, MP, FEAT),
            P(None, FEAT, MP),
            P(None, FEAT),
        ),
        check_vma=False,
    )
```

```python
import math

import jax
import jax.numpy as jnp
from jax import lax
from jax.sharding import Mesh, PartitionSpec as P

BF16 = jnp.bfloat16
F32 = jnp.float32
FEAT = ("y", "x", "zh")
MP = ("zl", "core")
RING = 4
ORDER = (0, 2, 1, 3)


def pair_index(source, target, layers):
    return source * (2 * layers - source + 1) // 2 + target - source


def shift(value, stage, by):
    if stage == "zh":
        return lax.ppermute(value, "zh", [(i, (i + by) % RING) for i in range(RING)])
    pairs = []
    for y in range(RING):
        for x in range(RING):
            for core in range(2):
                if (stage == "first") == (core == 0):
                    to = (y, (x + by) % RING)
                else:
                    to = ((y + by) % RING, x)
                pairs.append(((y * RING + x) * 2 + core, (to[0] * RING + to[1]) * 2 + core))
    return lax.ppermute(value, ("y", "x", "core"), pairs)


def swap(value, axis):
    return lax.ppermute(value, axis, [(0, 1), (1, 0)])


def flip(value):
    lead, rows, width = value.shape
    return value.reshape(lead, RING, RING, rows // RING**2, width).swapaxes(1, 2).reshape(value.shape)


def core_add(value):
    lead, rows, width = value.shape
    blocks = value.reshape(lead, RING**2, 2, rows // (2 * RING**2), width)
    me = lax.axis_index("core")
    mine = lax.dynamic_index_in_dim(blocks, me, 2, keepdims=False).reshape(lead, rows // 2, width)
    theirs = lax.dynamic_index_in_dim(blocks, 1 - me, 2, keepdims=False).reshape(lead, rows // 2, width)
    return mine.astype(F32) + flip(swap(theirs, "core")).astype(F32)


def core_join(value):
    lead, rows, width = value.shape
    got = flip(swap(value, "core"))
    first = lax.axis_index("core") == 0
    split = (lead, RING**2, 1, rows // RING**2, width)
    halves = [jnp.where(first, value, got).reshape(split), jnp.where(first, got, value).reshape(split)]
    return jnp.concatenate(halves, axis=2).reshape(lead, 2 * rows, width)


def chip_add(value):
    rows = value.shape[1] // 2
    me = lax.axis_index("zl")
    mine = lax.dynamic_slice_in_dim(value, me * rows, rows, 1)
    theirs = lax.dynamic_slice_in_dim(value, (1 - me) * rows, rows, 1)
    return mine.astype(F32) + swap(theirs, "zl").astype(F32)


def chip_join(value):
    got = swap(value, "zl")
    first = lax.axis_index("zl") == 0
    return jnp.concatenate([jnp.where(first, value, got), jnp.where(first, got, value)], axis=1)


def spread(value, stage):
    slots = {s: shift(value, stage, s) for s in ORDER[1:]}
    return jnp.concatenate([value] + [slots[s] for s in ORDER[1:]], axis=1)


def fold(value, stage):
    n = value.shape[1] // RING
    total = value[:, :n].astype(F32)
    for i in (2, 3, 1):
        piece = value[:, i * n : (i + 1) * n].astype(BF16)
        total = total + shift(piece, stage, -ORDER[i]).astype(F32)
    return total


def fold_all(value):
    blocks = (value.shape[0], RING, -1, value.shape[2])
    total = value.astype(F32).reshape(blocks)
    for s in ORDER[1:]:
        got = shift(value, "zh", s).reshape(blocks)
        back = [ORDER.index((ORDER[i] - s) % RING) for i in range(RING)]
        total = total + jnp.concatenate([got[:, i : i + 1] for i in back], axis=1).astype(F32)
    return total.reshape(value.shape)


def spread_wide(value):
    n = value.shape[1]
    slots = {s: shift(value, "second", s) for s in ORDER[1:]}
    full = jnp.zeros((value.shape[0], RING * n, value.shape[2]), value.dtype)
    full = lax.dynamic_update_slice_in_dim(full, value, 0, 1)
    for i in range(1, RING):
        full = lax.dynamic_update_slice_in_dim(full, slots[ORDER[i]], i * n, 1)
    return full


def on_device(acts_in, targets, enc_weight, enc_bias, dec_weight, dec_bias):
    layers = enc_weight.shape[0]
    acts_near = lax.optimization_barrier(spread(acts_in, "zh"))
    acts_first, targets_late = lax.optimization_barrier((spread(acts_near, "first"), targets))
    acts, targets_near = lax.optimization_barrier((spread_wide(acts_first), spread(targets_late, "zh")))
    loss_scale = 1.0 / math.sqrt(acts.shape[1])

    partial = jnp.einsum("ltd,ldf->ltf", acts, enc_weight, preferred_element_type=F32)
    pre_own = chip_add(core_add(partial)) + enc_bias[:, None, :]
    half_feature = chip_join(jnp.maximum(pre_own, 0.0).astype(BF16))
    feature = core_join(half_feature)

    totals = []
    for target in range(layers):
        total = 0.0
        for source in range(target + 1):
            total = total + jnp.dot(
                feature[source], dec_weight[pair_index(source, target, layers)], preferred_element_type=F32
            )
        totals.append(total.astype(BF16))
    part = fold(lax.optimization_barrier(fold(jnp.stack(totals), "second")), "first")
    recon = fold_all(part.astype(BF16))
    near = (recon + dec_bias[:, None, :] - targets_near.astype(F32)).astype(BF16)
    errors = near[:, : targets.shape[1]]
    near = near + swap(near[:, :1, :1], "core") * jnp.zeros((), BF16)
    err_all = spread_wide(lax.optimization_barrier(spread(near, "first")))

    grad_dec = {}
    grad_act = []
    for source in range(layers):
        total = 0.0
        for target in range(source, layers):
            pair = pair_index(source, target, layers)
            total = total + jnp.einsum("td,fd->tf", err_all[target], dec_weight[pair], preferred_element_type=F32)
            prod = jnp.einsum("tf,td->fd", feature[source], err_all[target], preferred_element_type=F32)
            grad_dec[pair] = (prod * loss_scale).astype(BF16)
        grad_act.append((total * loss_scale).astype(BF16))
    half = core_add(jnp.stack(grad_act)).astype(BF16)
    summed = half.astype(F32) + swap(half, "zl").astype(F32)
    grad_pre = core_join(jnp.where(half_feature > 0.0, summed, 0.0).astype(BF16))
    grad_enc = jnp.einsum("ltd,ltf->ldf", acts, grad_pre, preferred_element_type=F32).astype(BF16)
    grad_bias = jnp.sum(grad_pre.astype(F32), axis=1)
    return (errors, grad_enc, jnp.stack([grad_dec[pair] for pair in range(len(grad_dec))]), grad_bias)


def solution(mesh):
    fine = Mesh(mesh.devices.reshape(RING, RING, RING, 2, 2), FEAT + MP)
    return jax.shard_map(
        on_device,
        mesh=fine,
        in_specs=(
            P(None, FEAT, MP),
            P(None, FEAT, MP),
            P(None, MP, FEAT),
            P(None, FEAT),
            P(None, FEAT, MP),
            P(None, MP),
        ),
        out_specs=(
            P(None, FEAT, MP),
            P(None, MP, FEAT),
            P(None, FEAT, MP),
            P(None, FEAT),
        ),
        check_vma=False,
    )
```

```python
import math

import jax
import jax.numpy as jnp
from jax import lax
from jax.sharding import Mesh, PartitionSpec as P


BF16 = jnp.bfloat16
F32 = jnp.float32
FEAT = ("y", "x", "zh")
MP = ("zl", "core")
RING = 4
ORDER = (0, 2, 1, 3)


def pair_index(source, target, layers):
    return source * (2 * layers - source + 1) // 2 + target - source


def shift(value, stage, by):
    if stage == "zh":
        return lax.ppermute(value, "zh", [(i, (i + by) % RING) for i in range(RING)])
    pairs = []
    for y in range(RING):
        for x in range(RING):
            for core in range(2):
                if (stage == "first") == (core == 0):
                    to = (y, (x + by) % RING)
                else:
                    to = ((y + by) % RING, x)
                pairs.append(((y * RING + x) * 2 + core, (to[0] * RING + to[1]) * 2 + core))
    return lax.ppermute(value, ("y", "x", "core"), pairs)


def swap(value, axis):
    return lax.ppermute(value, axis, [(0, 1), (1, 0)])


def flip(value):
    lead, rows, width = value.shape
    return value.reshape(lead, RING, RING, rows // RING**2, width).swapaxes(1, 2).reshape(value.shape)


def core_add(value):
    lead, rows, width = value.shape
    blocks = value.reshape(lead, RING**2, 2, rows // (2 * RING**2), width)
    me = lax.axis_index("core")
    mine = lax.dynamic_index_in_dim(blocks, me, 2, keepdims=False).reshape(lead, rows // 2, width)
    theirs = lax.dynamic_index_in_dim(blocks, 1 - me, 2, keepdims=False).reshape(lead, rows // 2, width)
    return mine.astype(F32) + flip(swap(theirs, "core")).astype(F32)


def core_join(value):
    lead, rows, width = value.shape
    got = flip(swap(value, "core"))
    first = lax.axis_index("core") == 0
    split = (lead, RING**2, 1, rows // RING**2, width)
    halves = [jnp.where(first, value, got).reshape(split), jnp.where(first, got, value).reshape(split)]
    return jnp.concatenate(halves, axis=2).reshape(lead, 2 * rows, width)


def chip_add(value):
    rows = value.shape[1] // 2
    me = lax.axis_index("zl")
    mine = lax.dynamic_slice_in_dim(value, me * rows, rows, 1)
    theirs = lax.dynamic_slice_in_dim(value, (1 - me) * rows, rows, 1)
    return mine.astype(F32) + swap(theirs, "zl").astype(F32)


def chip_join(value):
    got = swap(value, "zl")
    first = lax.axis_index("zl") == 0
    return jnp.concatenate([jnp.where(first, value, got), jnp.where(first, got, value)], axis=1)


def spread(value, stage):
    slots = {s: shift(value, stage, s) for s in ORDER[1:]}
    return jnp.concatenate([value] + [slots[s] for s in ORDER[1:]], axis=1)


def fold(value, stage):
    n = value.shape[1] // RING
    total = value[:, :n].astype(F32)
    for i in (2, 3, 1):
        piece = value[:, i * n : (i + 1) * n].astype(BF16)
        total = total + shift(piece, stage, -ORDER[i]).astype(F32)
    return total


def gather_zh(value):
    copies = jnp.broadcast_to(value[None], (RING,) + value.shape)
    got = lax.optimization_barrier(lax.all_to_all(copies, "zh", split_axis=0, concat_axis=0, tiled=True))
    return jnp.moveaxis(got, 0, 1).reshape(value.shape[0], -1, value.shape[2])


def fold_all(value):
    total = value.astype(F32)
    for s in ORDER[1:]:
        total = total + shift(value, "zh", s).astype(F32)
    return total


def spread_wide(value):
    n = value.shape[1]
    slots = {s: shift(value, "second", s) for s in ORDER[1:]}
    full = jnp.zeros((value.shape[0], RING * n, value.shape[2]), value.dtype)
    full = lax.dynamic_update_slice_in_dim(full, value, 0, 1)
    for i in range(1, RING):
        full = lax.dynamic_update_slice_in_dim(full, slots[ORDER[i]], i * n, 1)
    return full


def on_device(acts_in, targets, enc_weight, enc_bias, dec_weight, dec_bias):
    layers = enc_weight.shape[0]
    near = gather_zh(jnp.concatenate([acts_in, targets], axis=0))
    targets_near = near[layers:]
    acts = spread_wide(lax.optimization_barrier(spread(near[:layers], "first")))
    loss_scale = 1.0 / math.sqrt(acts.shape[1])

    partial = jnp.einsum("ltd,ldf->ltf", acts, enc_weight, preferred_element_type=F32)
    pre_own = chip_add(core_add(partial)) + enc_bias[:, None, :]
    half_feature = chip_join(jnp.maximum(pre_own, 0.0).astype(BF16))
    feature = core_join(half_feature)

    totals = []
    for target in range(layers):
        total = 0.0
        for source in range(target + 1):
            total = total + jnp.dot(
                feature[source], dec_weight[pair_index(source, target, layers)], preferred_element_type=F32
            )
        totals.append(total.astype(BF16))
    part = fold(lax.optimization_barrier(fold(jnp.stack(totals), "second")), "first")
    recon = fold_all(part.astype(BF16))
    near = (recon + dec_bias[:, None, :] - targets_near.astype(F32)).astype(BF16)
    rows = targets.shape[1]
    errors = lax.dynamic_slice_in_dim(near, lax.axis_index("zh") * rows, rows, 1)
    near = near + swap(near[:, :1, :1], "core") * jnp.zeros((), BF16)
    err_first = lax.optimization_barrier(spread(near, "first"))
    late = spread_wide(err_first[1:])
    early = spread_wide(err_first[:1])
    err_all = [early[0]] + [late[i] for i in range(layers - 1)]

    grad_dec, grad_pre = {}, []
    for batch in (range(1, layers), range(1)):
        grad_act = []
        for source in batch:
            total = 0.0
            for target in range(source, layers):
                pair = pair_index(source, target, layers)
                total = total + jnp.einsum("td,fd->tf", err_all[target], dec_weight[pair], preferred_element_type=F32)
                prod = jnp.einsum("tf,td->fd", feature[source], err_all[target], preferred_element_type=F32)
                grad_dec[pair] = (prod * loss_scale).astype(BF16)
            grad_act.append((total * loss_scale).astype(BF16))
        half = core_add(jnp.stack(grad_act)).astype(BF16)
        other = swap(half, "zl")
        summed = half.astype(F32) + other.astype(F32)
        active = half_feature[batch.start : batch.stop] > 0.0
        grad_pre.append(core_join(jnp.where(active, summed, 0.0).astype(BF16)))
    grad_pre = jnp.concatenate(grad_pre[::-1], axis=0)
    grad_enc = jnp.einsum("ltd,ltf->ldf", acts, grad_pre, preferred_element_type=F32).astype(BF16)
    grad_bias = jnp.sum(grad_pre.astype(F32), axis=1)
    return (errors, grad_enc, jnp.stack([grad_dec[pair] for pair in range(len(grad_dec))]), grad_bias)


def solution(mesh):
    fine = Mesh(mesh.devices.reshape(RING, RING, RING, 2, 2), FEAT + MP)
    return jax.shard_map(
        on_device,
        mesh=fine,
        in_specs=(
            P(None, FEAT, MP),
            P(None, FEAT, MP),
            P(None, MP, FEAT),
            P(None, FEAT),
            P(None, FEAT, MP),
            P(None, MP),
        ),
        out_specs=(
            P(None, FEAT, MP),
            P(None, MP, FEAT),
            P(None, FEAT, MP),
            P(None, FEAT),
        ),
        check_vma=False,
    )
```

```python
import math

import jax
import jax.numpy as jnp
from jax import lax
from jax.sharding import Mesh, PartitionSpec as P


BF16 = jnp.bfloat16
F32 = jnp.float32
FEAT = ("y", "x", "zh")
MP = ("zl", "core")
RING = 4
ORDER = (0, 2, 1, 3)


def pair_index(source, target, layers):
    return source * (2 * layers - source + 1) // 2 + target - source


def shift(value, stage, by):
    if stage == "zh":
        return lax.ppermute(value, "zh", [(i, (i + by) % RING) for i in range(RING)])
    pairs = []
    for y in range(RING):
        for x in range(RING):
            for core in range(2):
                if (stage == "first") == (core == 0):
                    to = (y, (x + by) % RING)
                else:
                    to = ((y + by) % RING, x)
                pairs.append(((y * RING + x) * 2 + core, (to[0] * RING + to[1]) * 2 + core))
    return lax.ppermute(value, ("y", "x", "core"), pairs)


def swap(value, axis):
    return lax.ppermute(value, axis, [(0, 1), (1, 0)])


def flip(value):
    lead, rows, width = value.shape
    return value.reshape(lead, RING, RING, rows // RING**2, width).swapaxes(1, 2).reshape(value.shape)


def core_add(value):
    lead, rows, width = value.shape
    blocks = value.reshape(lead, RING**2, 2, rows // (2 * RING**2), width)
    me = lax.axis_index("core")
    mine = lax.dynamic_index_in_dim(blocks, me, 2, keepdims=False).reshape(lead, rows // 2, width)
    theirs = lax.dynamic_index_in_dim(blocks, 1 - me, 2, keepdims=False).reshape(lead, rows // 2, width)
    return mine.astype(F32) + flip(swap(theirs, "core")).astype(F32)


def core_join(value):
    lead, rows, width = value.shape
    got = flip(swap(value, "core"))
    first = lax.axis_index("core") == 0
    split = (lead, RING**2, 1, rows // RING**2, width)
    halves = [jnp.where(first, value, got).reshape(split), jnp.where(first, got, value).reshape(split)]
    return jnp.concatenate(halves, axis=2).reshape(lead, 2 * rows, width)


def chip_add(value):
    rows = value.shape[1] // 2
    me = lax.axis_index("zl")
    mine = lax.dynamic_slice_in_dim(value, me * rows, rows, 1)
    theirs = lax.dynamic_slice_in_dim(value, (1 - me) * rows, rows, 1)
    return mine.astype(F32) + swap(theirs, "zl").astype(F32)


def chip_join(value):
    got = swap(value, "zl")
    first = lax.axis_index("zl") == 0
    return jnp.concatenate([jnp.where(first, value, got), jnp.where(first, got, value)], axis=1)


def spread(value, stage):
    slots = {s: shift(value, stage, s) for s in ORDER[1:]}
    return jnp.concatenate([value] + [slots[s] for s in ORDER[1:]], axis=1)


def fold(value, stage):
    n = value.shape[1] // RING
    total = value[:, :n].astype(F32)
    for i in (2, 3, 1):
        piece = value[:, i * n : (i + 1) * n].astype(BF16)
        total = total + shift(piece, stage, -ORDER[i]).astype(F32)
    return total


def fold_all(value):
    blocks = (value.shape[0], RING, -1, value.shape[2])
    total = value.astype(F32).reshape(blocks)
    for s in ORDER[1:]:
        got = shift(value, "zh", s).reshape(blocks)
        back = [ORDER.index((ORDER[i] - s) % RING) for i in range(RING)]
        total = total + jnp.concatenate([got[:, i : i + 1] for i in back], axis=1).astype(F32)
    return total.reshape(value.shape)


def spread_wide(value):
    n = value.shape[1]
    slots = {s: shift(value, "second", s) for s in ORDER[1:]}
    full = jnp.zeros((value.shape[0], RING * n, value.shape[2]), value.dtype)
    full = lax.dynamic_update_slice_in_dim(full, value, 0, 1)
    for i in range(1, RING):
        full = lax.dynamic_update_slice_in_dim(full, slots[ORDER[i]], i * n, 1)
    return full


def on_device(acts_in, targets, enc_weight, enc_bias, dec_weight, dec_bias):
    layers = enc_weight.shape[0]
    near = lax.optimization_barrier(spread(jnp.concatenate([acts_in, targets], axis=0), "zh"))
    targets_near = near[layers:]
    acts = spread_wide(lax.optimization_barrier(spread(near[:layers], "first")))
    loss_scale = 1.0 / math.sqrt(acts.shape[1])

    partial = jnp.einsum("ltd,ldf->ltf", acts, enc_weight, preferred_element_type=F32)
    pre_own = chip_add(core_add(partial)) + enc_bias[:, None, :]
    half_feature = chip_join(jnp.maximum(pre_own, 0.0).astype(BF16))
    feature = core_join(half_feature)

    totals = jnp.zeros(acts.shape, BF16)
    for target in range(layers):
        total = 0.0
        for source in range(target + 1):
            total = total + jnp.dot(
                feature[source], dec_weight[pair_index(source, target, layers)], preferred_element_type=F32
            )
        totals = lax.dynamic_update_slice(totals, total.astype(BF16)[None], (target, 0, 0))
    part = fold(lax.optimization_barrier(fold(totals, "second")), "first")
    recon = fold_all(part.astype(BF16))
    near = (recon + dec_bias[:, None, :] - targets_near.astype(F32)).astype(BF16)
    errors = near[:, : targets.shape[1]]
    near = near + swap(near[:, :1, :1], "core") * jnp.zeros((), BF16)
    err_first = lax.optimization_barrier(spread(near, "first"))
    late = spread_wide(err_first[1:])
    early = spread_wide(err_first[:1])
    err_all = [early[0]] + [late[i] for i in range(layers - 1)]

    grad_dec, grad_pre = {}, []
    for batch in (range(1, layers), range(1)):
        grad_act = []
        for source in batch:
            total = 0.0
            for target in range(source, layers):
                pair = pair_index(source, target, layers)
                total = total + jnp.einsum("td,fd->tf", err_all[target], dec_weight[pair], preferred_element_type=F32)
                prod = jnp.einsum("tf,td->fd", feature[source], err_all[target], preferred_element_type=F32)
                grad_dec[pair] = (prod * loss_scale).astype(BF16)
            grad_act.append((total * loss_scale).astype(BF16))
        half = core_add(jnp.stack(grad_act)).astype(BF16)
        other = swap(half, "zl")
        summed = half.astype(F32) + other.astype(F32)
        active = half_feature[batch.start : batch.stop] > 0.0
        grad_pre.append(core_join(jnp.where(active, summed, 0.0).astype(BF16)))
    grad_pre = jnp.concatenate(grad_pre[::-1], axis=0)
    grad_enc = jnp.einsum("ltd,ltf->ldf", acts, grad_pre, preferred_element_type=F32).astype(BF16)
    grad_bias = jnp.sum(grad_pre.astype(F32), axis=1)
    return (errors, grad_enc, jnp.stack([grad_dec[pair] for pair in range(len(grad_dec))]), grad_bias)


def solution(mesh):
    fine = Mesh(mesh.devices.reshape(RING, RING, RING, 2, 2), FEAT + MP)
    return jax.shard_map(
        on_device,
        mesh=fine,
        in_specs=(
            P(None, FEAT, MP),
            P(None, FEAT, MP),
            P(None, MP, FEAT),
            P(None, FEAT),
            P(None, FEAT, MP),
            P(None, MP),
        ),
        out_specs=(
            P(None, FEAT, MP),
            P(None, MP, FEAT),
            P(None, FEAT, MP),
            P(None, FEAT),
        ),
        check_vma=False,
    )
```

```python
import math

import jax
import jax.numpy as jnp
from jax import lax
from jax.sharding import Mesh, PartitionSpec as P


BF16 = jnp.bfloat16
F32 = jnp.float32
FEAT = ("y", "x", "zh")
MP = ("zl", "core")
RING = 4
ORDER = (0, 2, 1, 3)


def pair_index(source, target, layers):
    return source * (2 * layers - source + 1) // 2 + target - source


def shift(value, stage, by):
    if stage == "zh":
        return lax.ppermute(value, "zh", [(i, (i + by) % RING) for i in range(RING)])
    pairs = []
    for y in range(RING):
        for x in range(RING):
            for core in range(2):
                if (stage == "first") == (core == 0):
                    to = (y, (x + by) % RING)
                else:
                    to = ((y + by) % RING, x)
                pairs.append(((y * RING + x) * 2 + core, (to[0] * RING + to[1]) * 2 + core))
    return lax.ppermute(value, ("y", "x", "core"), pairs)


def swap(value, axis):
    return lax.ppermute(value, axis, [(0, 1), (1, 0)])


def flip(value):
    lead, rows, width = value.shape
    return value.reshape(lead, RING, RING, rows // RING**2, width).swapaxes(1, 2).reshape(value.shape)


def core_add(value):
    lead, rows, width = value.shape
    blocks = value.reshape(lead, RING**2, 2, rows // (2 * RING**2), width)
    me = lax.axis_index("core")
    mine = lax.dynamic_index_in_dim(blocks, me, 2, keepdims=False).reshape(lead, rows // 2, width)
    theirs = lax.dynamic_index_in_dim(blocks, 1 - me, 2, keepdims=False).reshape(lead, rows // 2, width)
    return mine.astype(F32) + flip(swap(theirs, "core")).astype(F32)


def core_join(value):
    lead, rows, width = value.shape
    got = flip(swap(value, "core"))
    first = lax.axis_index("core") == 0
    split = (lead, RING**2, 1, rows // RING**2, width)
    halves = [jnp.where(first, value, got).reshape(split), jnp.where(first, got, value).reshape(split)]
    return jnp.concatenate(halves, axis=2).reshape(lead, 2 * rows, width)


def chip_add(value):
    rows = value.shape[1] // 2
    me = lax.axis_index("zl")
    mine = lax.dynamic_slice_in_dim(value, me * rows, rows, 1)
    theirs = lax.dynamic_slice_in_dim(value, (1 - me) * rows, rows, 1)
    return mine.astype(F32) + swap(theirs, "zl").astype(F32)


def chip_join(value):
    got = swap(value, "zl")
    first = lax.axis_index("zl") == 0
    return jnp.concatenate([jnp.where(first, value, got), jnp.where(first, got, value)], axis=1)


def in_step(value):
    return value + swap(value[:1, :1, :1], "core") * jnp.zeros((), value.dtype)


def spread(value, stage):
    slots = {s: shift(value, stage, s) for s in ORDER[1:]}
    return jnp.concatenate([value] + [slots[s] for s in ORDER[1:]], axis=1)


def fold(value, stage):
    n = value.shape[1] // RING
    total = value[:, :n].astype(F32)
    for i in (2, 3, 1):
        piece = value[:, i * n : (i + 1) * n].astype(BF16)
        total = total + shift(piece, stage, -ORDER[i]).astype(F32)
    return total


def fold_all(value):
    blocks = (value.shape[0], RING, -1, value.shape[2])
    total = value.astype(F32).reshape(blocks)
    for s in ORDER[1:]:
        got = shift(value, "zh", s).reshape(blocks)
        back = [ORDER.index((ORDER[i] - s) % RING) for i in range(RING)]
        total = total + jnp.concatenate([got[:, i : i + 1] for i in back], axis=1).astype(F32)
    return total.reshape(value.shape)


def spread_wide(value):
    n = value.shape[1]
    slots = {s: shift(value, "second", s) for s in ORDER[1:]}
    full = jnp.zeros((value.shape[0], RING * n, value.shape[2]), value.dtype)
    full = lax.dynamic_update_slice_in_dim(full, value, 0, 1)
    for i in range(1, RING):
        full = lax.dynamic_update_slice_in_dim(full, slots[ORDER[i]], i * n, 1)
    return full


def on_device(acts_in, targets, enc_weight, enc_bias, dec_weight, dec_bias):
    layers = enc_weight.shape[0]
    near = lax.optimization_barrier(spread(jnp.concatenate([acts_in, targets], axis=0), "zh"))
    targets_near = near[layers:]
    acts = spread_wide(lax.optimization_barrier(spread(near[:layers], "first")))
    loss_scale = 1.0 / math.sqrt(acts.shape[1])

    partial = jnp.einsum("ltd,ldf->ltf", acts, enc_weight, preferred_element_type=F32)
    pre_own = chip_add(core_add(partial)) + enc_bias[:, None, :]
    half_feature = chip_join(jnp.maximum(pre_own, 0.0).astype(BF16))
    feature = core_join(half_feature)

    totals = jnp.zeros(acts.shape, BF16)
    for target in range(layers):
        total = 0.0
        for source in range(target + 1):
            total = total + jnp.dot(
                feature[source], dec_weight[pair_index(source, target, layers)], preferred_element_type=F32
            )
        totals = lax.dynamic_update_slice(totals, total.astype(BF16)[None], (target, 0, 0))
    wide = in_step(fold(totals, "second").astype(BF16))
    part = fold(lax.optimization_barrier(wide), "first")
    recon = fold_all(part.astype(BF16))
    near = (recon + dec_bias[:, None, :] - targets_near.astype(F32)).astype(BF16)
    errors = near[:, : targets.shape[1]]
    err_first = lax.optimization_barrier(spread(near, "first"))
    late = spread_wide(err_first[1:])
    early = spread_wide(err_first[:1])
    err_all = [early[0]] + [late[i] for i in range(layers - 1)]

    grad_dec, grad_pre = {}, []
    for batch in (range(1, layers), range(1)):
        grad_act = []
        for source in batch:
            total = 0.0
            for target in range(source, layers):
                pair = pair_index(source, target, layers)
                total = total + jnp.einsum("td,fd->tf", err_all[target], dec_weight[pair], preferred_element_type=F32)
                prod = jnp.einsum("tf,td->fd", feature[source], err_all[target], preferred_element_type=F32)
                grad_dec[pair] = (prod * loss_scale).astype(BF16)
            grad_act.append((total * loss_scale).astype(BF16))
        half = core_add(jnp.stack(grad_act)).astype(BF16)
        other = swap(half, "zl")
        summed = half.astype(F32) + other.astype(F32)
        active = half_feature[batch.start : batch.stop] > 0.0
        grad_pre.append(core_join(jnp.where(active, summed, 0.0).astype(BF16)))
    grad_pre = jnp.concatenate(grad_pre[::-1], axis=0)
    grad_enc = jnp.einsum("ltd,ltf->ldf", acts, grad_pre, preferred_element_type=F32).astype(BF16)
    grad_bias = jnp.sum(grad_pre.astype(F32), axis=1)
    return (errors, grad_enc, jnp.stack([grad_dec[pair] for pair in range(len(grad_dec))]), grad_bias)


def solution(mesh):
    fine = Mesh(mesh.devices.reshape(RING, RING, RING, 2, 2), FEAT + MP)
    return jax.shard_map(
        on_device,
        mesh=fine,
        in_specs=(
            P(None, FEAT, MP),
            P(None, FEAT, MP),
            P(None, MP, FEAT),
            P(None, FEAT),
            P(None, FEAT, MP),
            P(None, MP),
        ),
        out_specs=(
            P(None, FEAT, MP),
            P(None, MP, FEAT),
            P(None, FEAT, MP),
            P(None, FEAT),
        ),
        check_vma=False,
    )
```

```python
import math

import jax
import jax.numpy as jnp
from jax import lax
from jax.sharding import Mesh, PartitionSpec as P


BF16 = jnp.bfloat16
F32 = jnp.float32
FEAT = ("y", "x", "zh")
MP = ("zl", "core")
RING = 4
ORDER = (0, 2, 1, 3)


def pair_index(source, target, layers):
    return source * (2 * layers - source + 1) // 2 + target - source


def shift(value, stage, by):
    if stage == "zh":
        return lax.ppermute(value, "zh", [(i, (i + by) % RING) for i in range(RING)])
    pairs = []
    for y in range(RING):
        for x in range(RING):
            for core in range(2):
                if (stage == "first") == (core == 0):
                    to = (y, (x + by) % RING)
                else:
                    to = ((y + by) % RING, x)
                pairs.append(((y * RING + x) * 2 + core, (to[0] * RING + to[1]) * 2 + core))
    return lax.ppermute(value, ("y", "x", "core"), pairs)


def swap(value, axis):
    return lax.ppermute(value, axis, [(0, 1), (1, 0)])


def flip(value):
    lead, rows, width = value.shape
    return value.reshape(lead, RING, RING, rows // RING**2, width).swapaxes(1, 2).reshape(value.shape)


def core_add(value):
    lead, rows, width = value.shape
    blocks = value.reshape(lead, RING**2, 2, rows // (2 * RING**2), width)
    me = lax.axis_index("core")
    mine = lax.dynamic_index_in_dim(blocks, me, 2, keepdims=False).reshape(lead, rows // 2, width)
    theirs = lax.dynamic_index_in_dim(blocks, 1 - me, 2, keepdims=False).reshape(lead, rows // 2, width)
    return mine.astype(F32) + flip(swap(theirs, "core")).astype(F32)


def core_join(value):
    lead, rows, width = value.shape
    got = flip(swap(value, "core"))
    first = lax.axis_index("core") == 0
    split = (lead, RING**2, 1, rows // RING**2, width)
    halves = [jnp.where(first, value, got).reshape(split), jnp.where(first, got, value).reshape(split)]
    return jnp.concatenate(halves, axis=2).reshape(lead, 2 * rows, width)


def chip_add(value):
    rows = value.shape[1] // 2
    me = lax.axis_index("zl")
    mine = lax.dynamic_slice_in_dim(value, me * rows, rows, 1)
    theirs = lax.dynamic_slice_in_dim(value, (1 - me) * rows, rows, 1)
    return mine.astype(F32) + swap(theirs, "zl").astype(F32)


def chip_join(value):
    got = swap(value, "zl")
    first = lax.axis_index("zl") == 0
    return jnp.concatenate([jnp.where(first, value, got), jnp.where(first, got, value)], axis=1)


def spread(value, stage):
    slots = {s: shift(value, stage, s) for s in ORDER[1:]}
    return jnp.concatenate([value] + [slots[s] for s in ORDER[1:]], axis=1)


def fold(value, stage):
    n = value.shape[1] // RING
    total = value[:, :n].astype(F32)
    for i in (2, 3, 1):
        piece = value[:, i * n : (i + 1) * n].astype(BF16)
        total = total + shift(piece, stage, -ORDER[i]).astype(F32)
    return total


def fold_all(value):
    blocks = (value.shape[0], RING, -1, value.shape[2])
    total = value.astype(F32).reshape(blocks)
    for s in ORDER[1:]:
        got = shift(value, "zh", s).reshape(blocks)
        back = [ORDER.index((ORDER[i] - s) % RING) for i in range(RING)]
        total = total + jnp.concatenate([got[:, i : i + 1] for i in back], axis=1).astype(F32)
    return total.reshape(value.shape)


def spread_wide(value):
    n = value.shape[1]
    slots = {s: shift(value, "second", s) for s in ORDER[1:]}
    full = jnp.zeros((value.shape[0], RING * n, value.shape[2]), value.dtype)
    full = lax.dynamic_update_slice_in_dim(full, value, 0, 1)
    for i in range(1, RING):
        full = lax.dynamic_update_slice_in_dim(full, slots[ORDER[i]], i * n, 1)
    return full


def on_device(acts_in, targets, enc_weight, enc_bias, dec_weight, dec_bias):
    layers = enc_weight.shape[0]
    acts = lax.optimization_barrier(spread(lax.optimization_barrier(spread(acts_in, "zh")), "first"))
    acts = spread_wide(acts)
    loss_scale = 1.0 / math.sqrt(acts.shape[1])

    partial = jnp.einsum("ltd,ldf->ltf", acts, enc_weight, preferred_element_type=F32)
    pre_own = chip_add(core_add(partial)) + enc_bias[:, None, :]
    half_feature = chip_join(jnp.maximum(pre_own, 0.0).astype(BF16))
    feature = core_join(half_feature)

    totals = jnp.zeros(acts.shape, BF16)
    for target in range(layers):
        total = 0.0
        for source in range(target + 1):
            total = total + jnp.dot(
                feature[source], dec_weight[pair_index(source, target, layers)], preferred_element_type=F32
            )
        totals = lax.dynamic_update_slice(totals, total.astype(BF16)[None], (target, 0, 0))
    wide = lax.optimization_barrier(fold(totals, "second").astype(BF16))
    part = fold(wide, "first")
    rows = targets.shape[1]
    own = part[:, :rows] + dec_bias[:, None, :] - targets.astype(F32)
    near = fold_all(jnp.concatenate([own, part[:, rows:]], axis=1).astype(BF16)).astype(BF16)
    errors = near[:, :rows]
    near = near + swap(near[:, :1, :1], "core") * jnp.zeros((), BF16)
    err_first = lax.optimization_barrier(spread(near, "first"))
    late = spread_wide(err_first[1:])
    early = spread_wide(err_first[:1])
    err_all = [early[0]] + [late[i] for i in range(layers - 1)]

    grad_dec, grad_pre = {}, []
    for batch in (range(1, layers), range(1)):
        grad_act = []
        for source in batch:
            total = 0.0
            for target in range(source, layers):
                pair = pair_index(source, target, layers)
                total = total + jnp.einsum("td,fd->tf", err_all[target], dec_weight[pair], preferred_element_type=F32)
                prod = jnp.einsum("tf,td->fd", feature[source], err_all[target], preferred_element_type=F32)
                grad_dec[pair] = (prod * loss_scale).astype(BF16)
            grad_act.append((total * loss_scale).astype(BF16))
        half = core_add(jnp.stack(grad_act)).astype(BF16)
        other = swap(half, "zl")
        summed = half.astype(F32) + other.astype(F32)
        active = half_feature[batch.start : batch.stop] > 0.0
        grad_pre.append(core_join(jnp.where(active, summed, 0.0).astype(BF16)))
    grad_pre = jnp.concatenate(grad_pre[::-1], axis=0)
    grad_enc = jnp.einsum("ltd,ltf->ldf", acts, grad_pre, preferred_element_type=F32).astype(BF16)
    grad_bias = jnp.sum(grad_pre.astype(F32), axis=1)
    return (errors, grad_enc, jnp.stack([grad_dec[pair] for pair in range(len(grad_dec))]), grad_bias)


def solution(mesh):
    fine = Mesh(mesh.devices.reshape(RING, RING, RING, 2, 2), FEAT + MP)
    return jax.shard_map(
        on_device,
        mesh=fine,
        in_specs=(
            P(None, FEAT, MP),
            P(None, FEAT, MP),
            P(None, MP, FEAT),
            P(None, FEAT),
            P(None, FEAT, MP),
            P(None, MP),
        ),
        out_specs=(
            P(None, FEAT, MP),
            P(None, MP, FEAT),
            P(None, FEAT, MP),
            P(None, FEAT),
        ),
        check_vma=False,
    )
```

```python
import math

import jax
import jax.numpy as jnp
from jax import lax
from jax.sharding import Mesh, PartitionSpec as P


BF16 = jnp.bfloat16
F32 = jnp.float32
FEAT = ("y", "x", "zh")
MP = ("zl", "core")
RING = 4
ORDER = (0, 2, 1, 3)


def pair_index(source, target, layers):
    return source * (2 * layers - source + 1) // 2 + target - source


def shift(value, stage, by):
    if stage == "zh":
        return lax.ppermute(value, "zh", [(i, (i + by) % RING) for i in range(RING)])
    pairs = []
    for y in range(RING):
        for x in range(RING):
            for core in range(2):
                if (stage == "first") == (core == 0):
                    to = (y, (x + by) % RING)
                else:
                    to = ((y + by) % RING, x)
                pairs.append(((y * RING + x) * 2 + core, (to[0] * RING + to[1]) * 2 + core))
    return lax.ppermute(value, ("y", "x", "core"), pairs)


def swap(value, axis):
    return lax.ppermute(value, axis, [(0, 1), (1, 0)])


def flip(value):
    lead, rows, width = value.shape
    return value.reshape(lead, RING, RING, rows // RING**2, width).swapaxes(1, 2).reshape(value.shape)


def core_add(value):
    rows = value.shape[1] // 2
    me = lax.axis_index("core")
    mine = lax.dynamic_slice_in_dim(value, me * rows, rows, 1)
    theirs = lax.dynamic_slice_in_dim(value, (1 - me) * rows, rows, 1)
    mine, theirs = lax.optimization_barrier((mine, theirs))
    return mine.astype(F32) + flip(swap(theirs, "core")).astype(F32)


def core_join(value):
    got = flip(swap(value, "core"))
    first = lax.axis_index("core") == 0
    return jnp.concatenate([jnp.where(first, value, got), jnp.where(first, got, value)], axis=1)


def by_half(value):
    return value.reshape(value.shape[0] * 2, value.shape[1] // 2, value.shape[2])


def by_layer(value):
    return value.reshape(value.shape[0] // 2, value.shape[1] * 2, value.shape[2])


def chip_add(value):
    rows = value.shape[1] // 2
    me = lax.axis_index("zl")
    mine = lax.dynamic_slice_in_dim(value, me * rows, rows, 1)
    theirs = lax.dynamic_slice_in_dim(value, (1 - me) * rows, rows, 1)
    return mine.astype(F32) + swap(theirs, "zl").astype(F32)


def chip_join(value):
    got = swap(value, "zl")
    first = lax.axis_index("zl") == 0
    return jnp.concatenate([jnp.where(first, value, got), jnp.where(first, got, value)], axis=1)


def spread(value, stage):
    slots = {s: shift(value, stage, s) for s in ORDER[1:]}
    return jnp.concatenate([value] + [slots[s] for s in ORDER[1:]], axis=1)


def fold(value, stage):
    n = value.shape[1] // RING
    total = value[:, :n].astype(F32)
    for i in (2, 3, 1):
        piece = value[:, i * n : (i + 1) * n].astype(BF16)
        total = total + shift(piece, stage, -ORDER[i]).astype(F32)
    return total


def fold_all(value):
    blocks = (value.shape[0], RING, -1, value.shape[2])
    total = value.astype(F32).reshape(blocks)
    for s in ORDER[1:]:
        got = shift(value, "zh", s).reshape(blocks)
        back = [ORDER.index((ORDER[i] - s) % RING) for i in range(RING)]
        total = total + jnp.concatenate([got[:, i : i + 1] for i in back], axis=1).astype(F32)
    return total.reshape(value.shape)


def spread_wide(value):
    n = value.shape[1]
    slots = {s: shift(value, "second", s) for s in ORDER[1:]}
    full = jnp.zeros((value.shape[0], RING * n, value.shape[2]), value.dtype)
    full = lax.dynamic_update_slice_in_dim(full, value, 0, 1)
    for i in range(1, RING):
        full = lax.dynamic_update_slice_in_dim(full, slots[ORDER[i]], i * n, 1)
    return full


def on_device(acts_in, targets, enc_weight, enc_bias, dec_weight, dec_bias):
    layers = enc_weight.shape[0]
    acts = by_half(lax.optimization_barrier(spread(acts_in, "zh")))
    acts = by_layer(spread_wide(lax.optimization_barrier(spread(acts, "first"))))
    loss_scale = 1.0 / math.sqrt(acts.shape[1])

    partial = jnp.einsum("ltd,ldf->ltf", acts, enc_weight, preferred_element_type=F32)
    pre_own = chip_add(core_add(partial)) + enc_bias[:, None, :]
    half_feature = chip_join(jnp.maximum(pre_own, 0.0).astype(BF16))
    feature = core_join(half_feature)

    totals = jnp.zeros(acts.shape, BF16)
    for target in range(layers):
        total = 0.0
        for source in range(target + 1):
            total = total + jnp.dot(
                feature[source], dec_weight[pair_index(source, target, layers)], preferred_element_type=F32
            )
        totals = lax.dynamic_update_slice(totals, total.astype(BF16)[None], (target, 0, 0))
    wide = lax.optimization_barrier(fold(by_half(totals), "second").astype(BF16))
    part = by_layer(fold(wide, "first"))
    rows = targets.shape[1]
    own = part[:, :rows] + dec_bias[:, None, :] - targets.astype(F32)
    near = fold_all(jnp.concatenate([own, part[:, rows:]], axis=1).astype(BF16)).astype(BF16)
    errors = near[:, :rows]
    near = lax.optimization_barrier(near)
    in_step = swap(near[0, :8, :128], "core")[0, 0] * jnp.zeros((), BF16)
    err_first = lax.optimization_barrier(spread(by_half(near) + in_step, "first"))
    late = by_layer(spread_wide(err_first[2:]))
    early = by_layer(spread_wide(err_first[:2]))
    err_all = [early[0]] + [late[i] for i in range(layers - 1)]

    grad_dec, grad_pre = {}, []
    for batch in (range(1, layers), range(1)):
        grad_act = []
        for source in batch:
            total = 0.0
            for target in range(source, layers):
                pair = pair_index(source, target, layers)
                total = total + jnp.einsum("td,fd->tf", err_all[target], dec_weight[pair], preferred_element_type=F32)
                prod = jnp.einsum("tf,td->fd", feature[source], err_all[target], preferred_element_type=F32)
                grad_dec[pair] = (prod * loss_scale).astype(BF16)
            grad_act.append((total * loss_scale).astype(BF16))
        half = core_add(jnp.stack(grad_act)).astype(BF16)
        other = swap(half, "zl")
        summed = half.astype(F32) + other.astype(F32)
        active = half_feature[batch.start : batch.stop] > 0.0
        grad_pre.append(core_join(jnp.where(active, summed, 0.0).astype(BF16)))
    grad_pre = jnp.concatenate(grad_pre[::-1], axis=0)
    grad_enc = jnp.einsum("ltd,ltf->ldf", acts, grad_pre, preferred_element_type=F32).astype(BF16)
    grad_bias = jnp.sum(grad_pre.astype(F32), axis=1)
    return (errors, grad_enc, jnp.stack([grad_dec[pair] for pair in range(len(grad_dec))]), grad_bias)


def solution(mesh):
    fine = Mesh(mesh.devices.reshape(RING, RING, RING, 2, 2), FEAT + MP)
    return jax.shard_map(
        on_device,
        mesh=fine,
        in_specs=(
            P(None, FEAT, MP),
            P(None, FEAT, MP),
            P(None, MP, FEAT),
            P(None, FEAT),
            P(None, FEAT, MP),
            P(None, MP),
        ),
        out_specs=(
            P(None, FEAT, MP),
            P(None, MP, FEAT),
            P(None, FEAT, MP),
            P(None, FEAT),
        ),
        check_vma=False,
    )
```
